256 devices in a mesh: grid: 128 (over z, y, x_hi, core), orb: 2 (over x_lo).
Axes of the slice: x: 4 (x_hi: 2, x_lo: 2; x = x_hi * 2 + x_lo), y: 4, z: 8, core: 2. Of those that a mesh axis runs over, the one named last changes fastest.
Arguments:
- density: float32 [256, 3, 128, 128], P('grid', None, 'orb'), may hold values from -4 to 4
- basis_values: float32 [256, 1280, 768], P(('grid', 'orb')), may hold values from -0.5 to 0.5
- quad_weights: float32 [256, 1280], P(('grid', 'orb')), may hold values from 0.01 to 0.1
- ext_potential: float32 [256, 1280], P(('grid', 'orb')), may hold values from 0 to 4
- batch_blocks: int32 [256, 6], P(('grid', 'orb')), may hold values from 0 to 255, as said below
- domain_blocks: int32 [512, 4], P(('grid', 'orb')), may hold values from 0 to 255, as said below
- coefficients: float32 [512, 4, 128, 128], P(('grid', 'orb')), may hold values from -0.25 to 0.25
Outputs:
- density_out: float32 [256, 3, 128, 128], P('grid', None, 'orb')
- coefficients_out: float32 [512, 4, 128, 128], P(('grid', 'orb'))
The draws below stay inside these ranges and needn't reach their ends.
Inputs may be any that keep to these rules, and one draw needn't show every extreme that they name: `batch_blocks`: the batches on grid index g (batch numbers g * 256 / 128 onward) list the 6 blocks from (g - 1) * 2 onward, taken modulo 256, each once, in some order. `domain_blocks`: the domains on grid index g list 4 distinct blocks among the 6 blocks from (g - 1) * 2 onward, taken modulo 256, at least one of the first 2 and one of the last 2 of them.
All inputs are finite; a program needn't handle non-finite values.
Results may differ from the reference program's by a relative error of at most 0.0003.
Values sent between devices are 32-bit elements; how exact they have to be, the bound alone decides.
A program may use at most 64 MiB of HBM per device.

```python
import math
import jax
import jax.numpy as jnp
from jax import lax

NB = 128
BF = 6
DB = 4
PTS = 1280
FB = 2
ITERS = 2
NFB = 256
NBATCH = 256
NDOM = 512


def draw_block_lists(key, rows, count):
    subkeys = jax.random.split(key, 3)
    first_pick = jax.random.randint(subkeys[0], (rows, 1), 0, FB)
    last_pick = jax.random.randint(subkeys[1], (rows, 1), 2 * FB, 3 * FB)
    shuffled = jax.vmap(lambda row_key: jax.random.permutation(row_key, 3 * FB))(jax.random.split(subkeys[2], rows))
    positions = jnp.arange(3 * FB, dtype=jnp.int32)[None, :]
    scores = jnp.where(positions == first_pick, -2, jnp.where(positions == last_pick, -1, shuffled.astype(jnp.int32)))
    chosen = jnp.argsort(scores, axis=1, stable=True)[:, :count].astype(jnp.int32)
    owner_grid = jnp.arange(rows, dtype=jnp.int32) // (rows // (NFB // FB))
    return jnp.mod(owner_grid[:, None] * FB - FB + chosen, NFB).astype(jnp.int32)


def draw_batch_blocks(key, part):
    return draw_block_lists(jax.random.fold_in(key, 11), NBATCH, BF)


def draw_domain_blocks(key, part):
    return draw_block_lists(jax.random.fold_in(key, 23), NDOM, DB)


def block_scale(own_key, extent, shards, smallest, largest):
    factor_of, own = 1.0, jax.random.fold_in(own_key, 6)
    for axis_at, shards_of in shards:
        draws = jnp.exp(jax.random.uniform(jax.random.fold_in(own, axis_at), (shards_of,), jnp.float32, smallest / len(shards), largest / len(shards)))
        factor_of = factor_of * jnp.repeat(draws, extent[axis_at] // shards_of).reshape([-1 if axis == axis_at else 1 for axis in range(len(extent))])
    return factor_of


def normal_values(own_key, dims, spread, most, pieces=(), kind=jnp.bfloat16):
    gain = block_scale(own_key, dims, pieces, -0.22, 0.18) if pieces else 1.0
    entries = jax.random.normal(own_key, dims, jnp.float32) * spread * gain
    return jnp.minimum(jnp.maximum(entries, -most), most).astype(kind)


def setup_inputs(seed: int = 0) -> dict:
    seeds = jax.random.split(jax.random.key(seed), 8)
    return {
        "density": normal_values(seeds[0], (NFB, 3, NB, NB), 0.25, 4.0, ((0, 128), (2, 2)), jnp.float32),
        "basis_values": normal_values(seeds[1], (NBATCH, PTS, BF * NB), NB ** -0.5, 0.5, ((0, 256),), jnp.float32),
        "quad_weights": jnp.clip(jnp.exp(math.log(0.1) - 2.3025851 * jax.random.uniform(seeds[2], (NBATCH, PTS), jnp.float32) ** block_scale(seeds[2], (NBATCH, PTS), ((0, 256),), -0.2, 0.2)), 0.01, 0.1),
        "ext_potential": jnp.clip(4.0 * jax.random.uniform(seeds[3], (NBATCH, PTS), jnp.float32) ** block_scale(seeds[3], (NBATCH, PTS), ((0, 256),), -0.2, 0.2), 0.0, 4.0),
        "batch_blocks": draw_batch_blocks(jax.random.fold_in(seeds[7], 71), 0),
        "domain_blocks": draw_domain_blocks(jax.random.fold_in(seeds[7], 71), 0),
        "coefficients": normal_values(seeds[6], (NDOM, DB, NB, NB), (DB * NB) ** -0.5, 0.25, ((0, 256),), jnp.float32),
    }


step_scale = 0.5


def pair_index(blocks, anchor, total_blocks):
    relative = jnp.mod(blocks - anchor, total_blocks)
    offset = jnp.mod(blocks[None, :] - blocks[:, None] + 1, total_blocks)
    inside = offset <= 2
    positions = relative[:, None] * 3 + jnp.where(inside, offset, 0)
    return positions, inside


def gather_tiles(flat_band, positions, inside):
    return jnp.where(inside[..., None, None], flat_band[positions], 0.0)


def place_tiles(flat_band, positions, inside, block_tiles):
    masked = jnp.where(inside[..., None, None], block_tiles, 0.0)
    rows = masked.reshape(-1, block_tiles.shape[-2], block_tiles.shape[-1])
    return flat_band.at[positions.reshape(-1)].add(rows)


def batch_fock(basis, weights, external, block_tiles):
    count_blocks = block_tiles.shape[0]
    block_size = block_tiles.shape[2]
    width = count_blocks * block_size
    batch_density = block_tiles.transpose(0, 2, 1, 3).reshape(width, width)
    projected = jnp.dot(basis, batch_density, precision=lax.Precision.HIGHEST, preferred_element_type=jnp.float32)
    density_points = jnp.sum(projected * basis, axis=1)
    potential = external - jnp.power(density_points * density_points + 1.0, 1.0 / 6.0)
    scaled = basis * (weights * potential)[:, None]
    fock_tiles = jnp.einsum("pm,pn->mn", scaled, basis, precision=lax.Precision.HIGHEST)
    return fock_tiles.reshape(count_blocks, block_size, count_blocks, block_size).transpose(0, 2, 1, 3)


def domain_update(fock_blocks, current):
    gradient = jnp.einsum("ijab,jbc->iac", fock_blocks, current, precision=lax.Precision.HIGHEST)
    intersection = jnp.einsum("iab,iac->bc", current, gradient, precision=lax.Precision.HIGHEST)
    updated = current - step_scale * (gradient - jnp.einsum("iab,bc->iac", current, intersection, precision=lax.Precision.HIGHEST))
    outer_terms = jnp.einsum("iab,jcb->ijac", updated, updated, precision=lax.Precision.HIGHEST)
    return updated, outer_terms


def reference(density, basis_values, quad_weights, ext_potential, batch_blocks, domain_blocks, coefficients):
    band_blocks = density
    current = coefficients
    for iteration in range(ITERS):
        flat_band = band_blocks.reshape(-1, NB, NB)

        def per_batch(accumulated, element):
            basis, weights, external, blocks = element
            positions, inside = pair_index(blocks, 0, NFB)
            block_tiles = gather_tiles(flat_band, positions, inside)
            fock_tiles = batch_fock(basis, weights, external, block_tiles)
            return place_tiles(accumulated, positions, inside, fock_tiles), 0.0

        fock_flat, ignored = lax.scan(per_batch, jnp.zeros_like(flat_band), (basis_values, quad_weights, ext_potential, batch_blocks))

        def per_domain(accumulated, element):
            blocks, domain_coef = element
            positions, inside = pair_index(blocks, 0, NFB)
            updated, outer_terms = domain_update(gather_tiles(fock_flat, positions, inside), domain_coef)
            return place_tiles(accumulated, positions, inside, outer_terms), updated

        new_flat, current = lax.scan(per_domain, jnp.zeros_like(flat_band), (domain_blocks, current))
        band_blocks = new_flat.reshape(NFB, 3, NB, NB)
    return band_blocks, current
```

```python
import functools

import jax
import jax.numpy as jnp
from jax import lax
from jax.experimental import pallas as pl
from jax.experimental.pallas import tpu as pltpu
from jax.sharding import PartitionSpec as P

ITERS = 2
STEP_SCALE = 0.5
WIN = 6
F32 = jnp.float32
BF16 = jnp.bfloat16

DIAG = (0, 1, 4, 5, 8, 9)
PAIR_OFF = (2, 6, 10)
CROSS_OFF = (3, 7)
FULL_PAIR = ((0, 1, 2, 3), (6, 7, 8, 9), (12, 13, 14, 15))
FULL_CROSS = ((4, 5), (10, 11))


def split(value):
    high = value.astype(BF16)
    return high, (value - high.astype(F32)).astype(BF16)


def mul(a, b):
    return lax.dot_general(a, b, (((1,), (0,)), ((), ())), preferred_element_type=F32)


def mul_nt(a, b):
    return lax.dot_general(a, b, (((1,), (1,)), ((), ())), preferred_element_type=F32)


def mul3(a, b, product=mul):
    (ah, al), (bh, bl) = a, b
    return product(ah, bh) + (product(ah, bl) + product(al, bh))


def kernel(
    count,
    dens_ref, basis_hbm, quad_ref, ext_ref, batch_ref, domain_ref, coef_ref,
    dens_out, coef_out,
    basis_ref, basis_high, basis_low, scaled_high, scaled_low,
    pair_high, pair_low, cross_high, cross_low,
    coef_now, grad_now, full_win, full_part, full_recv,
    parts, recvs, owns, wins,
    basis_sem, send_sems, recv_sems,
):
    block = coef_ref.shape[2]
    half = block // 2
    points = basis_ref.shape[0]
    domains, listed = coef_ref.shape[:2]
    g = lax.axis_index("grid")
    o = lax.axis_index("orb")
    after = lax.rem(g + 1, count)
    before = lax.rem(g + count - 1, count)
    other = 1 - o
    targets = ((g, other), (after, o), (after, other), (before, o), (before, other))
    mine = pl.ds(pl.multiple_of(o * half, half), half)
    theirs = pl.ds(pl.multiple_of(other * half, half), half)

    fetch = pltpu.make_async_copy(basis_hbm, basis_ref, basis_sem)
    fetch.start()

    barrier = pltpu.get_barrier_semaphore()
    for to_grid, to_orb in targets:
        pl.semaphore_signal(
            barrier, inc=1, device_id=(to_grid, to_orb), device_id_type=pl.DeviceIdType.MESH
        )
    pl.semaphore_wait(barrier, len(targets))

    started = []

    def send(phase, k, source, target):
        copy = pltpu.make_async_remote_copy(
            src_ref=source,
            dst_ref=target,
            send_sem=send_sems.at[phase, k],
            recv_sem=recv_sems.at[phase, k],
            device_id=targets[k],
            device_id_type=pl.DeviceIdType.MESH,
        )
        copy.start()
        started.append(copy)
        return copy

    arriving = [
        send(0, k, dens_ref.at[pl.ds(a, size)], full_win.at[pl.ds(b, size), mine])
        for k, a, size, b in ((3, 0, 5, 11), (4, 0, 5, 11), (1, 1, 5, 0), (2, 1, 5, 0), (0, 0, 6, 5))
    ]
    full_win[5:11, mine] = dens_ref[...]

    total = 2 * count
    anchor = 2 * g - 2

    def position(value):
        return lax.rem(value - anchor + total, total)

    batch_at = [position(batch_ref[0, j]) for j in range(WIN)]
    domain_at = [[position(domain_ref[d, j]) for j in range(listed)] for d in range(domains)]

    def hit(at, w):
        return jnp.maximum(1 - jnp.abs(at - w), 0).astype(F32)

    batch_hits = [[hit(at, w) for at in batch_at] for w in range(WIN)]
    domain_hits = [[[hit(at, w) for at in places] for w in range(WIN)] for places in domain_at]

    def picked(pieces, weights):
        total_of = pieces[0] * weights[0]
        for piece, weight in zip(pieces[1:], weights[1:]):
            total_of = total_of + piece * weight
        return total_of

    masks = [[sum(hits[1:], hits[0]) for hits in by_window] for by_window in domain_hits]
    for d in range(domains):
        for w in range(WIN):
            coef_now[w * block : (w + 1) * block, d * block : (d + 1) * block] = picked(
                [coef_ref[d, j] for j in range(listed)], domain_hits[d][w]
            )

    fetch.wait()
    for w in range(WIN):
        values = picked(
            [basis_ref[:, j * block : (j + 1) * block] for j in range(WIN)], batch_hits[w]
        )
        high, low = split(values.T)
        basis_high[w * block : (w + 1) * block, :] = high
        basis_low[w * block : (w + 1) * block, :] = low

    def rows(w, size=1):
        return slice(w * block, (w + size) * block)

    def set_pair(t, value):
        pair_high[t], pair_low[t] = split(value)

    def set_cross(t, value):
        cross_high[t], cross_low[t] = split(value)

    def joined(aa, ab, ba, bb):
        return jnp.concatenate(
            [jnp.concatenate([aa, ab], axis=1), jnp.concatenate([ba, bb], axis=1)], axis=0
        )

    def density_from_full():
        for t in range(3):
            value = joined(*(full_win[s] for s in FULL_PAIR[t]))
            set_pair(t, 0.5 * (value + value.T))
        for t in range(2):
            upper, lower = FULL_CROSS[t]
            set_cross(t, full_win[upper].T + full_win[lower])

    def load_pairs(win):
        for t in range(3):
            off = win[PAIR_OFF[t]]
            set_pair(t, joined(win[DIAG[2 * t]], off, off.T, win[DIAG[2 * t + 1]]))

    def density_from_window(win):
        load_pairs(win)
        for t in range(2):
            set_cross(t, 2.0 * win[CROSS_OFF[t]].T)

    def potential_step():
        tile = 2 * block

        def step(i, carry):
            lanes = pl.ds(pl.multiple_of(i * tile, tile), tile)
            rho = jnp.zeros((1, tile), F32)
            weighted = []
            for t in range(3):
                high = basis_high[rows(2 * t, 2), lanes]
                twice = high.astype(F32) + 2.0 * basis_low[rows(2 * t, 2), lanes].astype(F32)
                image = mul(pair_high[t], high) + mul(pair_low[t], high)
                rho = rho + jnp.sum(image * twice, axis=0, keepdims=True)
                weighted.append(twice)
            for t in range(2):
                source, sink = rows(2 * t + 1), rows(2 * t + 2)
                high, low = basis_high[source, lanes], basis_low[source, lanes]
                image = mul3((cross_high[t], cross_low[t]), (high, low))
                values = basis_high[sink, lanes].astype(F32) + basis_low[sink, lanes].astype(F32)
                rho = rho + jnp.sum(image * values, axis=0, keepdims=True)
            potential = ext_ref[:, lanes] - jnp.exp(jnp.log(rho * rho + 1.0) * (1.0 / 6.0))
            scale = quad_ref[:, lanes] * potential
            for t in range(3):
                high, low = split(weighted[t] * scale)
                scaled_high[rows(2 * t, 2), lanes] = high
                scaled_low[rows(2 * t, 2), lanes] = low
            return carry

        lax.fori_loop(0, points // tile, step, 0)

    def fock_part(left, right):
        return mul_nt(basis_high[left, :], scaled_high[right, :]) + mul_nt(
            basis_high[left, :], scaled_low[right, :]
        )

    def put_pair(part, t, value):
        part[DIAG[2 * t]] = value[:block, :block]
        part[DIAG[2 * t + 1]] = value[block:, block:]
        part[PAIR_OFF[t]] = value[:block, block:]

    def fock_pair(part, t):
        value = fock_part(rows(2 * t, 2), rows(2 * t, 2))
        put_pair(part, t, 0.5 * (value + value.T))

    def fock_cross(part, t):
        low, high = rows(2 * t + 1), rows(2 * t + 2)
        part[CROSS_OFF[t]] = 0.5 * (fock_part(low, high) + fock_part(high, low).T)

    def outer_pair(values, t):
        high, low = values
        at = rows(2 * t, 2)
        return mul3((high[at], low[at]), (high[at], low[at]), mul_nt)

    def outer_block(values, left, right):
        high, low = values
        left, right = rows(left), rows(right)
        return mul3((high[left], low[left]), (high[right], low[right]), mul_nt)

    def reduce_and_gather(index, make_pair, make_cross):
        part, recv, own, win = parts.at[index], recvs.at[index], owns.at[index], wins.at[index]
        phase = 1 + 2 * index
        make_pair(part, 0)
        make_cross(part, 0)
        coming = {}
        for k, to_rows in ((3, mine), (4, theirs)):
            coming[k] = send(phase, k, part.at[pl.ds(0, 4), to_rows], recv.at[k, pl.ds(0, 4)])
        make_pair(part, 2)
        for k, to_rows in ((1, mine), (2, theirs)):
            coming[k] = send(phase, k, part.at[pl.ds(8, 3), to_rows], recv.at[k, pl.ds(0, 3)])
        make_pair(part, 1)
        make_cross(part, 1)
        coming[0] = send(phase, 0, part.at[pl.ds(4, 4), theirs], recv.at[0, pl.ds(0, 4)])
        for k in range(5):
            coming[k].wait_recv()
        own[0:3] = part[4:7, mine] + ((recv[0, 0:3] + recv[1, 0:3]) + (recv[2, 0:3] + (recv[3, 0:3] + recv[4, 0:3])))
        own[3] = part[7, mine] + (recv[0, 3] + (recv[3, 3] + recv[4, 3]))
        coming = [
            send(phase + 1, k, own.at[pl.ds(0, size)], win.at[pl.ds(b, size), mine])
            for k, size, b in ((3, 3, 8), (4, 3, 8), (1, 4, 0), (2, 4, 0), (0, 4, 4))
        ]
        win[4:8, mine] = own[...]
        for copy in coming:
            copy.wait_recv()
        return win

    def domain_step(win):
        load_pairs(win)
        for t in range(2):
            set_cross(t, win[CROSS_OFF[t]])
        current = coef_now[...]
        now = split(current)
        for t in range(3):
            at = rows(2 * t, 2)
            grad_now[at] = mul3((pair_high[t], pair_low[t]), (now[0][at], now[1][at]))
        for t in range(2):
            low, high = rows(2 * t + 1), rows(2 * t + 2)
            factor = (cross_high[t], cross_low[t])
            grad_now[low] = grad_now[low] + mul3(factor, (now[0][high], now[1][high]))
            turned = split(win[CROSS_OFF[t]].T)
            grad_now[high] = grad_now[high] + mul3(turned, (now[0][low], now[1][low]))
        for d in range(domains):
            lanes = slice(d * block, (d + 1) * block)
            for w in range(WIN):
                grad_now[rows(w), lanes] = grad_now[rows(w), lanes] * masks[d][w]
            grad = grad_now[:, lanes]
            own = current[:, lanes]
            overlap = mul3(split(own.T), split(grad))
            back = mul3((now[0][:, lanes], now[1][:, lanes]), split(overlap))
            coef_now[:, lanes] = own - STEP_SCALE * (grad - back)

    win = None
    for iteration in range(ITERS):
        if iteration == 0:
            for copy in arriving:
                copy.wait_recv()
            density_from_full()
        else:
            density_from_window(win)
        potential_step()
        win = reduce_and_gather(2 * iteration, fock_pair, fock_cross)
        domain_step(win)
        values = split(coef_now[...])
        if iteration + 1 < ITERS:
            win = reduce_and_gather(
                2 * iteration + 1,
                lambda part, t: put_pair(part, t, outer_pair(values, t)),
                lambda part, t: part.__setitem__(CROSS_OFF[t], outer_block(values, 2 * t + 1, 2 * t + 2)),
            )

    def put_full_pair(t):
        value = outer_pair(values, t)
        aa, ab, ba, bb = FULL_PAIR[t]
        full_part[aa] = value[:block, :block]
        full_part[ab] = value[:block, block:]
        full_part[ba] = value[block:, :block]
        full_part[bb] = value[block:, block:]

    def put_full_cross(t):
        upper, lower = FULL_CROSS[t]
        value = outer_block(values, 2 * t + 1, 2 * t + 2)
        full_part[upper] = value
        full_part[lower] = value.T

    phase = send_sems.shape[0] - 1
    coming = {}
    put_full_pair(0)
    put_full_cross(0)
    for k, to_rows in ((3, mine), (4, theirs)):
        coming[k] = send(phase, k, full_part.at[pl.ds(0, 5), to_rows], full_recv.at[k, pl.ds(1, 5)])
    put_full_pair(2)
    put_full_cross(1)
    for k, to_rows in ((1, mine), (2, theirs)):
        coming[k] = send(phase, k, full_part.at[pl.ds(11, 5), to_rows], full_recv.at[k, pl.ds(0, 5)])
    put_full_pair(1)
    coming[0] = send(phase, 0, full_part.at[pl.ds(5, 6), theirs], full_recv.at[0, pl.ds(0, 6)])
    for d in range(domains):
        for j in range(listed):
            coef_out[d, j] = picked(
                [coef_now[rows(w), d * block : (d + 1) * block] for w in range(WIN)],
                [domain_hits[d][w][j] for w in range(WIN)],
            )
    for k in range(5):
        coming[k].wait_recv()
    for s in range(6):
        value = full_part[5 + s, mine] + full_recv[0, s]
        if s < 5:
            value = value + (full_recv[1, s] + full_recv[2, s])
        if s > 0:
            value = value + (full_recv[3, s] + full_recv[4, s])
        dens_out[s] = value
    for copy in started:
        copy.wait_send()


def shards(
    density, basis_values, quad_weights, ext_potential, batch_blocks, domain_blocks, coefficients
):
    own_blocks, offsets, half, block = density.shape
    points, width = basis_values.shape[1:]
    domains, listed = coefficients.shape[:2]
    sums = 2 * ITERS - 1
    vmem = pl.BlockSpec(memory_space=pltpu.VMEM)
    smem = pl.BlockSpec(memory_space=pltpu.SMEM)
    dens, coef = pl.pallas_call(
        functools.partial(kernel, lax.axis_size("grid")),
        out_shape=(
            jax.ShapeDtypeStruct((own_blocks * offsets, half, block), F32),
            jax.ShapeDtypeStruct(coefficients.shape, F32),
        ),
        in_specs=[vmem, pl.BlockSpec(memory_space=pl.ANY), vmem, vmem, smem, smem, vmem],
        out_specs=(vmem, vmem),
        scratch_shapes=[
            pltpu.VMEM((points, width), F32),
            pltpu.VMEM((width, points), BF16),
            pltpu.VMEM((width, points), BF16),
            pltpu.VMEM((width, points), BF16),
            pltpu.VMEM((width, points), BF16),
            pltpu.VMEM((3, 2 * block, 2 * block), BF16),
            pltpu.VMEM((3, 2 * block, 2 * block), BF16),
            pltpu.VMEM((2, block, block), BF16),
            pltpu.VMEM((2, block, block), BF16),
            pltpu.VMEM((width, domains * block), F32),
            pltpu.VMEM((width, domains * block), F32),
            pltpu.VMEM((16, block, block), F32),
            pltpu.VMEM((16, block, block), F32),
            pltpu.VMEM((5, 6, half, block), F32),
            pltpu.VMEM((sums, 11, block, block), F32),
            pltpu.VMEM((sums, 5, 4, half, block), F32),
            pltpu.VMEM((sums, 4, half, block), F32),
            pltpu.VMEM((sums, 11, block, block), F32),
            pltpu.SemaphoreType.DMA,
            pltpu.SemaphoreType.DMA((2 * sums + 2, 5)),
            pltpu.SemaphoreType.DMA((2 * sums + 2, 5)),
        ],
        compiler_params=pltpu.CompilerParams(collective_id=0, has_side_effects=True),
    )(
        density.reshape(own_blocks * offsets, half, block),
        basis_values[0],
        quad_weights,
        ext_potential,
        batch_blocks,
        domain_blocks,
        coefficients,
    )
    return dens.reshape(density.shape), coef


def solution(mesh):
    in_specs = (
        P("grid", None, "orb", None),
        P(("grid", "orb"), None, None),
        P(("grid", "orb"), None),
        P(("grid", "orb"), None),
        P(("grid", "orb"), None),
        P(("grid", "orb"), None),
        P(("grid", "orb"), None, None, None),
    )
    out_specs = (P("grid", None, "orb", None), P(("grid", "orb"), None, None, None))
    return jax.shard_map(shards, mesh=mesh, in_specs=in_specs, out_specs=out_specs, check_vma=False)
```

```python
import functools

import jax
import jax.numpy as jnp
from jax import lax
from jax.experimental import pallas as pl
from jax.experimental.pallas import tpu as pltpu
from jax.sharding import PartitionSpec as P

ITERS = 2
STEP_SCALE = 0.5
WIN = 6
F32 = jnp.float32
BF16 = jnp.bfloat16

FULL_CROSS = ((4, 5), (10, 11))


def split(value):
    high = value.astype(BF16)
    return high, (value - high.astype(F32)).astype(BF16)


def mul(a, b):
    return lax.dot_general(a, b, (((1,), (0,)), ((), ())), preferred_element_type=F32)


def mul_nt(a, b):
    return lax.dot_general(a, b, (((1,), (1,)), ((), ())), preferred_element_type=F32)


def mul3(a, b, product=mul):
    (ah, al), (bh, bl) = a, b
    return product(ah, bh) + (product(ah, bl) + product(al, bh))


def kernel(
    count,
    dens_ref, basis_hbm, quad_ref, ext_ref, batch_ref, domain_ref, coef_ref,
    dens_out, coef_out,
    basis_ref, basis_high, basis_low, basis_twice, scaled_high, scaled_low, rho_ref,
    pair_high, pair_low, cross_high, cross_low,
    coef_now, coef_high, coef_low, grad_now,
    full_win, full_part, full_far, full_sib, full_orb,
    parts, far_recvs, sib_recvs, orb_recvs, owns, wins,
    basis_sem, send_sems, recv_sems,
):
    block = coef_ref.shape[2]
    half = block // 2
    points = basis_ref.shape[0]
    domains, listed = coef_ref.shape[:2]
    g = lax.axis_index("grid")
    o = lax.axis_index("orb")
    parity = lax.rem(g, 2)
    sib = g + 1 - 2 * parity
    far = lax.rem(g + count - 1 + 2 * parity, count)
    other = 1 - o
    ORB, SIB, FAR, FAR_CROSS, RELAY = range(5)
    partners = ((g, other), (sib, o), (far, o), (far, other))
    target_of = partners + (partners[SIB],)
    mine = pl.ds(pl.multiple_of(o * half, half), half)
    theirs = pl.ds(pl.multiple_of(other * half, half), half)

    fetch = pltpu.make_async_copy(basis_hbm, basis_ref, basis_sem)
    fetch.start()
    for index in range(parts.shape[0]):
        sib_recvs[index, 3] = jnp.zeros((block, block), F32)
        for k in range(2):
            far_recvs[index, k, 3] = jnp.zeros((half, block), F32)

    barrier = pltpu.get_barrier_semaphore()
    for partner in partners:
        pl.semaphore_signal(
            barrier, inc=1, device_id=partner, device_id_type=pl.DeviceIdType.MESH
        )
    pl.semaphore_wait(barrier, len(partners))

    sent = {None: [], 0: [], 1: []}

    def describe(phase, k, source, target):
        return pltpu.make_async_remote_copy(
            src_ref=source,
            dst_ref=target,
            send_sem=send_sems.at[phase, k],
            recv_sem=recv_sems.at[phase, k],
            device_id=target_of[k],
            device_id_type=pl.DeviceIdType.MESH,
        )

    def send(phase, k, source, target, when=None):
        describe(phase, k, source, target).start()
        sent[when].append((phase, k, source.shape))

    def await_arrival(phase, k, target):
        describe(phase, k, target, target).wait_recv()

    def by_parity(action):
        for p in range(2):
            pl.when(parity == p)(functools.partial(action, p))

    total = 2 * count
    anchor = 2 * g - 2

    def position(value):
        return lax.rem(value - anchor + total, total)

    def hit(at, w):
        return jnp.maximum(1 - jnp.abs(at - w), 0).astype(F32)

    def picked(pieces, weights):
        total_of = pieces[0] * weights[0]
        for piece, weight in zip(pieces[1:], weights[1:]):
            total_of = total_of + piece * weight
        return total_of

    def rows(w, size=1):
        return slice(w * block, (w + size) * block)

    def pair_rows(t):
        if isinstance(t, int):
            return rows(2 * t, 2)
        return pl.ds(pl.multiple_of(t * 2 * block, 2 * block), 2 * block)

    t_far, t_sib = 2 * parity, 2 - 2 * parity

    sib_from, far_from = 1 - parity, parity
    sib_to, far_to = 11 * parity, 11 * (1 - parity)
    send(0, FAR, dens_ref.at[pl.ds(far_from, 5)], full_win.at[pl.ds(far_to, 5), mine])
    send(0, FAR_CROSS, dens_ref.at[pl.ds(far_from, 5)], full_win.at[pl.ds(far_to, 5), mine])
    send(0, ORB, dens_ref, full_win.at[pl.ds(5, 6), mine])
    send(0, SIB, dens_ref.at[pl.ds(sib_from, 5)], full_win.at[pl.ds(sib_to, 5), mine])
    full_win[5:11, mine] = dens_ref[...]

    batch_hits = []
    for w in range(WIN):
        batch_hits.append([hit(position(batch_ref[0, j]), w) for j in range(WIN)])
    domain_hits = []
    for d in range(domains):
        places = [position(domain_ref[d, j]) for j in range(listed)]
        domain_hits.append([[hit(at, w) for at in places] for w in range(WIN)])
    masks = [[sum(hits[1:], hits[0]) for hits in by_window] for by_window in domain_hits]

    def sort_basis(w):
        values = picked(
            [basis_ref[:, j * block : (j + 1) * block] for j in range(WIN)], batch_hits[w]
        )
        high, low = split(values.T)
        basis_high[rows(w), :] = high
        basis_low[rows(w), :] = low
        basis_twice[rows(w), :] = high.astype(F32) + 2.0 * low.astype(F32)

    def sort_coefficients():
        for d in range(domains):
            for w in range(WIN):
                coef_now[rows(w), d * block : (d + 1) * block] = picked(
                    [coef_ref[d, j] for j in range(listed)], domain_hits[d][w]
                )

    fetch.wait()
    for w in range(WIN):
        sort_basis(w)

    def set_pair(t, value):
        pair_high[t], pair_low[t] = split(value)

    def set_cross(t, value):
        cross_high[t], cross_low[t] = split(value)

    def joined(aa, ab, ba, bb):
        return jnp.concatenate(
            [jnp.concatenate([aa, ab], axis=1), jnp.concatenate([ba, bb], axis=1)], axis=0
        )

    def full_pair(t):
        value = joined(*(full_win[6 * t + s] for s in range(4)))
        set_pair(t, 0.5 * (value + value.T))

    def full_cross(t):
        upper, lower = FULL_CROSS[t]
        set_cross(t, full_win[upper].T + full_win[lower])

    def window_pair(win, t):
        off = win[4 * t + 2]
        set_pair(t, joined(win[4 * t], off, off.T, win[4 * t + 1]))

    tile = 2 * block

    def over_points(step):
        def at_tile(i, carry):
            step(pl.ds(pl.multiple_of(i * tile, tile), tile))
            return carry

        lax.fori_loop(0, points // tile, at_tile, 0)

    def rho_pair(t, lanes):
        high = basis_high[pair_rows(t), lanes]
        image = mul(pair_high[t], high) + mul(pair_low[t], high)
        return jnp.sum(image * basis_twice[pair_rows(t), lanes], axis=0, keepdims=True)

    def rho_cross(t, lanes):
        source, sink = rows(2 * t + 1), rows(2 * t + 2)
        image = mul3(
            (cross_high[t], cross_low[t]), (basis_high[source, lanes], basis_low[source, lanes])
        )
        values = basis_high[sink, lanes].astype(F32) + basis_low[sink, lanes].astype(F32)
        return jnp.sum(image * values, axis=0, keepdims=True)

    def rho_own(lanes):
        rho_ref[:, lanes] = rho_pair(1, lanes) + rho_cross(1, lanes)

    def rho_sib(lanes):
        rho_ref[:, lanes] = rho_ref[:, lanes] + rho_pair(t_sib, lanes)

    def rho_far(lanes, crosses=(0,)):
        rho = rho_ref[:, lanes] + rho_pair(t_far, lanes)
        for t in crosses:
            rho = rho + rho_cross(t, lanes)
        potential = ext_ref[:, lanes] - jnp.exp(jnp.log(rho * rho + 1.0) * (1.0 / 6.0))
        scale = quad_ref[:, lanes] * potential
        for t in range(3):
            high, low = split(basis_twice[pair_rows(t), lanes] * scale)
            scaled_high[pair_rows(t), lanes] = high
            scaled_low[pair_rows(t), lanes] = low

    def fock_part(left, right):
        return mul_nt(basis_high[left, :], scaled_high[right, :]) + mul_nt(
            basis_high[left, :], scaled_low[right, :]
        )

    def put_pair(part, t, value):
        part[4 * t] = value[:block, :block]
        part[4 * t + 1] = value[block:, block:]
        part[4 * t + 2] = value[:block, block:]

    def fock_pair(part, t):
        value = fock_part(pair_rows(t), pair_rows(t))
        put_pair(part, t, 0.5 * (value + value.T))

    def fock_cross(part, t):
        low, high = rows(2 * t + 1), rows(2 * t + 2)
        part[4 * t + 3] = 0.5 * (fock_part(low, high) + fock_part(high, low).T)

    def outer(left, right):
        return mul3(
            (coef_high[left, :], coef_low[left, :]), (coef_high[right, :], coef_low[right, :]), mul_nt
        )

    def outer_pair(part, t):
        put_pair(part, t, outer(pair_rows(t), pair_rows(t)))

    def outer_cross(part, t):
        part[4 * t + 3] = outer(rows(2 * t + 1), rows(2 * t + 2))

    def gathered(phase, win, groups, on_own, on_sib, on_far):
        await_arrival(phase, ORB, win.at[groups["own"], theirs])
        groups["relay"](phase, win)
        on_own()
        groups["sib"](phase, win)
        on_sib()
        groups["far"](phase, win)
        on_far()

    BEFORE, OWN, AFTER = pl.ds(0, 4), pl.ds(4, 4), pl.ds(8, 3)
    group_of_sib = (AFTER, BEFORE)
    group_of_far = (BEFORE, AFTER)
    size_for_sib = (4, 3)
    size_for_far = (3, 4)

    def relay(phase, win):
        by_parity(lambda p: send(
            phase, RELAY,
            win.at[pl.ds(4, size_for_sib[p]), theirs],
            win.at[group_of_sib[1 - p], theirs], p,
        ))

    def sib_arrival(phase, win):
        def action(p):
            await_arrival(phase, SIB, win.at[group_of_sib[p], mine])
            await_arrival(phase, RELAY, win.at[group_of_sib[p], theirs])
        by_parity(action)

    def far_arrival(phase, win):
        def action(p):
            await_arrival(phase, FAR, win.at[group_of_far[p], mine])
            await_arrival(phase, FAR_CROSS, win.at[group_of_far[p], theirs])
        by_parity(action)

    unique_groups = dict(own=OWN, relay=relay, sib=sib_arrival, far=far_arrival)

    def full_relay(phase, win):
        send(
            phase, RELAY,
            win.at[pl.ds(5 + sib_from, 5), theirs], win.at[pl.ds(sib_to, 5), theirs],
        )

    def full_sib_arrival(phase, win):
        await_arrival(phase, SIB, win.at[pl.ds(11 * (1 - parity), 5), mine])
        await_arrival(phase, RELAY, win.at[pl.ds(11 * (1 - parity), 5), theirs])

    def full_far_arrival(phase, win):
        await_arrival(phase, FAR, win.at[pl.ds(11 * parity, 5), mine])
        await_arrival(phase, FAR_CROSS, win.at[pl.ds(11 * parity, 5), theirs])

    full_groups = dict(
        own=pl.ds(5, 6), relay=full_relay, sib=full_sib_arrival, far=full_far_arrival
    )

    def reduce_and_gather(index, make_pair, make_cross, meanwhile, on_own, on_sib, on_far):
        part, own, win = parts.at[index], owns.at[index], wins.at[index]
        far_recv, sib_recv, orb_recv = far_recvs.at[index], sib_recvs.at[index], orb_recvs.at[index]
        phase = 1 + 2 * index
        make_pair(part, t_far)
        make_cross(part, 0)

        def to_far(p):
            at = group_of_far[p]
            send(phase, FAR, part.at[at, mine], far_recv.at[0, pl.ds(0, at.size)], p)
            send(phase, FAR_CROSS, part.at[at, theirs], far_recv.at[1, pl.ds(0, at.size)], p)

        by_parity(to_far)
        make_pair(part, t_sib)

        def to_sib(p):
            at = group_of_sib[p]
            send(phase, SIB, part.at[at], sib_recv.at[pl.ds(0, at.size)], p)

        by_parity(to_sib)
        make_pair(part, 1)
        make_cross(part, 1)
        by_parity(lambda p: await_arrival(phase, SIB, sib_recv.at[pl.ds(0, size_for_sib[p])]))
        part[4:8] = part[4:8] + sib_recv[...]
        send(phase, ORB, part.at[pl.ds(4, 4), theirs], orb_recv)
        meanwhile()
        await_arrival(phase, ORB, orb_recv)

        def from_far(p):
            for k in range(2):
                await_arrival(phase, FAR + k, far_recv.at[k, pl.ds(0, size_for_far[p])])

        by_parity(from_far)
        own[...] = (part[4:8, mine] + orb_recv[...]) + (far_recv[0] + far_recv[1])

        def give(p):
            for k in range(2):
                send(
                    phase + 1, FAR + k,
                    own.at[pl.ds(0, size_for_far[p])], win.at[group_of_far[1 - p], mine], p,
                )

        by_parity(give)
        send(phase + 1, ORB, own, win.at[OWN, mine])
        by_parity(lambda p: send(
            phase + 1, SIB, own.at[pl.ds(0, size_for_sib[p])], win.at[group_of_sib[1 - p], mine], p
        ))
        win[4:8, mine] = own[...]
        gathered(phase + 1, win, unique_groups, *(functools.partial(f, win) for f in (on_own, on_sib, on_far)))

    def grad_pair(win, t):
        window_pair(win, t)
        at = pair_rows(t)
        grad_now[at, :] = grad_now[at, :] + mul3(
            (pair_high[t], pair_low[t]), (coef_high[at, :], coef_low[at, :])
        )

    def grad_cross(win, t):
        low, high = rows(2 * t + 1), rows(2 * t + 2)
        value = win[4 * t + 3]
        grad_now[low, :] = grad_now[low, :] + mul3(
            split(value), (coef_high[high, :], coef_low[high, :])
        )
        grad_now[high, :] = grad_now[high, :] + mul3(
            split(value.T), (coef_high[low, :], coef_low[low, :])
        )

    def split_coefficients():
        coef_high[...], coef_low[...] = split(coef_now[...])
        grad_now[...] = jnp.zeros_like(grad_now)

    def grad_own(win):
        grad_pair(win, 1)
        grad_cross(win, 1)

    def grad_sib(win):
        grad_pair(win, t_sib)

    def grad_far(win):
        grad_pair(win, t_far)
        grad_cross(win, 0)
        for d in range(domains):
            lanes = slice(d * block, (d + 1) * block)
            for w in range(WIN):
                grad_now[rows(w), lanes] = grad_now[rows(w), lanes] * masks[d][w]
            grad = grad_now[:, lanes]
            own = coef_now[:, lanes]
            overlap = mul3(split(own.T), split(grad))
            back = mul3((coef_high[:, lanes], coef_low[:, lanes]), split(overlap))
            coef_now[:, lanes] = own - STEP_SCALE * (grad - back)

    def density_own(win):
        window_pair(win, 1)
        set_cross(1, 2.0 * win[7].T)
        over_points(rho_own)

    def density_sib(win):
        window_pair(win, t_sib)
        over_points(rho_sib)

    def density_far(win):
        window_pair(win, t_far)
        set_cross(0, 2.0 * win[3].T)
        over_points(rho_far)

    def rho_first(lanes):
        rho_ref[:, lanes] = rho_pair(1, lanes)

    def first_own():
        full_pair(1)
        over_points(rho_first)

    def first_sib():
        full_pair(t_sib)
        over_points(rho_sib)

    def first_far():
        full_pair(t_far)
        full_cross(0)
        full_cross(1)
        over_points(functools.partial(rho_far, crosses=(0, 1)))

    def nothing():
        pass

    gathered(0, full_win, full_groups, first_own, first_sib, first_far)
    for iteration in range(ITERS):

        def before_gradient():
            if iteration == 0:
                sort_coefficients()
                split_coefficients()
            else:
                grad_now[...] = jnp.zeros_like(grad_now)

        reduce_and_gather(
            2 * iteration, fock_pair, fock_cross, before_gradient, grad_own, grad_sib, grad_far
        )
        coef_high[...], coef_low[...] = split(coef_now[...])
        if iteration + 1 < ITERS:
            reduce_and_gather(
                2 * iteration + 1, outer_pair, outer_cross, nothing,
                density_own, density_sib, density_far,
            )

    def put_full_pair(t):
        value = outer(pair_rows(t), pair_rows(t))
        full_part[6 * t] = value[:block, :block]
        full_part[6 * t + 1] = value[:block, block:]
        full_part[6 * t + 2] = value[block:, :block]
        full_part[6 * t + 3] = value[block:, block:]

    def put_full_cross(t):
        upper, lower = FULL_CROSS[t]
        value = outer(rows(2 * t + 1), rows(2 * t + 2))
        full_part[upper] = value
        full_part[lower] = value.T

    phase = send_sems.shape[0] - 1
    at_far, at_sib = pl.ds(11 * parity, 5), pl.ds(11 * (1 - parity), 5)
    put_full_pair(t_far)
    put_full_cross(0)
    put_full_cross(1)
    send(phase, FAR, full_part.at[at_far, mine], full_far.at[0])
    send(phase, FAR_CROSS, full_part.at[at_far, theirs], full_far.at[1])
    put_full_pair(t_sib)
    send(phase, SIB, full_part.at[at_sib], full_sib)
    put_full_pair(1)
    await_arrival(phase, SIB, full_sib)
    joint = pl.ds(5 + sib_from, 5)
    full_part[joint] = full_part[joint] + full_sib[...]
    send(phase, ORB, full_part.at[pl.ds(5, 6), theirs], full_orb)
    for d in range(domains):
        for j in range(listed):
            coef_out[d, j] = picked(
                [coef_now[rows(w), d * block : (d + 1) * block] for w in range(WIN)],
                [domain_hits[d][w][j] for w in range(WIN)],
            )
    await_arrival(phase, ORB, full_orb)
    dens_out[...] = full_part[5:11, mine] + full_orb[...]
    await_arrival(phase, FAR, full_far.at[0])
    await_arrival(phase, FAR_CROSS, full_far.at[1])
    joint = pl.ds(far_from, 5)
    dens_out[joint] = dens_out[joint] + (full_far[0] + full_far[1])

    def finish(p):
        for phase, k, (size, height, _) in sent[p]:
            amount = parts.at[0, pl.ds(0, size), pl.ds(0, height)]
            describe(phase, k, amount, amount).wait_send()

    finish(None)
    by_parity(finish)


def shards(
    density, basis_values, quad_weights, ext_potential, batch_blocks, domain_blocks, coefficients
):
    own_blocks, offsets, half, block = density.shape
    points, width = basis_values.shape[1:]
    domains, listed = coefficients.shape[:2]
    sums = 2 * ITERS - 1
    vmem = pl.BlockSpec(memory_space=pltpu.VMEM)
    smem = pl.BlockSpec(memory_space=pltpu.SMEM)
    dens, coef = pl.pallas_call(
        functools.partial(kernel, lax.axis_size("grid")),
        out_shape=(
            jax.ShapeDtypeStruct((own_blocks * offsets, half, block), F32),
            jax.ShapeDtypeStruct(coefficients.shape, F32),
        ),
        in_specs=[vmem, pl.BlockSpec(memory_space=pl.ANY), vmem, vmem, smem, smem, vmem],
        out_specs=(vmem, vmem),
        scratch_shapes=[
            pltpu.VMEM((points, width), F32),
            pltpu.VMEM((width, points), BF16),
            pltpu.VMEM((width, points), BF16),
            pltpu.VMEM((width, points), F32),
            pltpu.VMEM((width, points), BF16),
            pltpu.VMEM((width, points), BF16),
            pltpu.VMEM((1, points), F32),
            pltpu.VMEM((3, 2 * block, 2 * block), BF16),
            pltpu.VMEM((3, 2 * block, 2 * block), BF16),
            pltpu.VMEM((2, block, block), BF16),
            pltpu.VMEM((2, block, block), BF16),
            pltpu.VMEM((width, domains * block), F32),
            pltpu.VMEM((width, domains * block), BF16),
            pltpu.VMEM((width, domains * block), BF16),
            pltpu.VMEM((width, domains * block), F32),
            pltpu.VMEM((16, block, block), F32),
            pltpu.VMEM((16, block, block), F32),
            pltpu.VMEM((2, 5, half, block), F32),
            pltpu.VMEM((5, block, block), F32),
            pltpu.VMEM((6, half, block), F32),
            pltpu.VMEM((sums, 11, block, block), F32),
            pltpu.VMEM((sums, 2, 4, half, block), F32),
            pltpu.VMEM((sums, 4, block, block), F32),
            pltpu.VMEM((sums, 4, half, block), F32),
            pltpu.VMEM((sums, 4, half, block), F32),
            pltpu.VMEM((sums, 11, block, block), F32),
            pltpu.SemaphoreType.DMA,
            pltpu.SemaphoreType.DMA((2 * sums + 2, 5)),
            pltpu.SemaphoreType.DMA((2 * sums + 2, 5)),
        ],
        compiler_params=pltpu.CompilerParams(collective_id=0, has_side_effects=True),
    )(
        density.reshape(own_blocks * offsets, half, block),
        basis_values[0],
        quad_weights,
        ext_potential,
        batch_blocks,
        domain_blocks,
        coefficients,
    )
    return dens.reshape(density.shape), coef


def solution(mesh):
    in_specs = (
        P("grid", None, "orb", None),
        P(("grid", "orb"), None, None),
        P(("grid", "orb"), None),
        P(("grid", "orb"), None),
        P(("grid", "orb"), None),
        P(("grid", "orb"), None),
        P(("grid", "orb"), None, None, None),
    )
    out_specs = (P("grid", None, "orb", None), P(("grid", "orb"), None, None, None))
    return jax.shard_map(shards, mesh=mesh, in_specs=in_specs, out_specs=out_specs, check_vma=False)
```
